32 devices in a mesh: dp: 8 (over y, x, core), shard: 4 (over z).
Axes of the slice: x: 2, y: 2, z: 4, core: 2. Of those that a mesh axis runs over, the one named last changes fastest.
Arguments:
- activations: bfloat16 [4096, 4096], P('dp', 'shard'), may hold values from -6 to 6
- out_grads: bfloat16 [4096, 14336], P('dp', 'shard'), may hold values from -6 to 6
- sign_bits: int32 [14336], P('shard'), may hold values from 0 to 1
- block_ids: int32 [4, 8], replicated, may hold values from 0 to 111, as said below
Outputs:
- gram: float32 [4096, 1024], P('shard')
The draws below stay inside these ranges and needn't reach their ends.
Inputs may be any that keep to these rules, and one draw needn't show every extreme that they name: `block_ids`: row o holds 4 runs of 2 entries; the entries of a run are distinct blocks of one shard s (ids s * 28 + 0 to s * 28 + 27), and the runs of a row come from distinct shards.
All inputs are finite; a program needn't handle non-finite values.
Results may differ from the reference program's by a relative error of at most 0.006.
Values may be sent and summed in bfloat16 or wider, within the bound.
A program may use at most 64 MiB of HBM per device.

```python
import math
import jax
import jax.numpy as jnp
from jax import lax

D = 4096
FF = 14336
BLK = 128
CAP = 2
GROUPS = 4
TOK = 512
BPS = 28
NBLK = 112
OWN_BLOCKS = 8
OWN = 1024
ROWS = 4096
N_DP = 8
N_SHARD = 4


def draw_block_ids(key, part):
    key_hot, key_pick, key_order = jax.random.split(key, 3)
    hot_shards = jax.random.randint(key_hot, (N_SHARD,), 0, 2)
    pick_noise = jax.random.randint(key_pick, (N_SHARD, N_SHARD), 0, 8)
    shard_scores = (pick_noise + 4 * hot_shards[None, :]) * N_SHARD + jnp.arange(N_SHARD, dtype=jnp.int32)[None, :]
    unused, sources = lax.top_k(shard_scores, GROUPS)
    order_scores = jax.random.randint(key_order, (N_SHARD, GROUPS, BPS), 0, 1 << 20) * BPS + jnp.arange(BPS, dtype=jnp.int32)
    local_ids = jnp.argsort(order_scores, axis=-1)[:, :, :CAP]
    return (sources[:, :, None] * BPS + local_ids).reshape(N_SHARD, GROUPS * CAP).astype(jnp.int32)


def plant(entries, key, low, high):
    longest = entries.shape.index(max(entries.shape))
    spots = []
    for shift in (0, 1):
        where = [jax.random.randint(jax.random.fold_in(key, axis), (), 0, length) for axis, length in enumerate(entries.shape)]
        where[longest] = (where[longest] + shift) % entries.shape[longest]
        spots.append(tuple(where))
    return entries.at[spots[0]].set(low).at[spots[1]].set(high)


def block_levels(key, dims, cuts, low, largest):
    level, own = 1.0, jax.random.fold_in(key, 6)
    for dim, parts in cuts:
        steps = jnp.exp(jax.random.uniform(jax.random.fold_in(own, dim), (parts,), jnp.float32, low / len(cuts), largest / len(cuts)))
        level = level * jnp.repeat(steps, dims[dim] // parts).reshape([-1 if axis == dim else 1 for axis in range(len(dims))])
    return level


def gaussian(key, dims, scale, most, shards=(), kind=jnp.bfloat16):
    values = scale * jax.random.normal(key, dims, jnp.float32)
    if shards:
        values = values * block_levels(key, dims, shards, -0.22, 0.18)
    return jnp.clip(values, -most, most).astype(kind)


def setup_inputs(seed: int = 0) -> dict:
    splits = jax.random.split(jax.random.key(seed), 5)
    return {
        "activations": gaussian(splits[0], (ROWS, D), 1.0, 6.0, ((0, 8), (1, 4))),
        "out_grads": gaussian(splits[1], (ROWS, FF), 1.0, 6.0, ((0, 8), (1, 4))),
        "sign_bits": plant(jax.random.randint(splits[2], (FF,), 0, 2), jax.random.fold_in(splits[2], 1), 0, 1).astype(jnp.int32),
        "block_ids": draw_block_ids(jax.random.fold_in(splits[4], 71), 0),
    }


def parity_table(count):
    index = jnp.arange(count, dtype=jnp.int32)
    total = jnp.zeros((count, count), jnp.int32)
    for level in range(count.bit_length() - 1):
        total = total + (jnp.right_shift(index[:, None], level) & jnp.right_shift(index[None, :], level) & 1)
    return (1 - 2 * (total % 2)).astype(jnp.float32)

def reference(activations, out_grads, sign_bits, block_ids):
    highest = lax.Precision.HIGHEST
    block_table = parity_table(BLK)
    shard_table = parity_table(N_SHARD)
    sign_values = (1 - 2 * sign_bits).astype(jnp.bfloat16)
    seq_acts = activations.reshape(N_DP, TOK, D)
    seq_grads = out_grads.reshape(N_DP, TOK, FF)

    def accumulate(running, example_pair):
        example_acts, example_grads = example_pair
        token_gram = jnp.dot(example_acts, example_acts.T, preferred_element_type=jnp.float32).astype(jnp.bfloat16)
        flipped = (example_grads * sign_values[None, :]).reshape(TOK, N_SHARD, BPS, BLK)
        local_mix = jnp.einsum('tsbj,jk->tsbk', flipped.astype(jnp.float32), block_table, precision=highest)
        local_mix = (local_mix * (1.0 / math.sqrt(BLK))).astype(jnp.bfloat16)
        mixed = jnp.einsum('rs,tsbk->rbtk', shard_table, local_mix.astype(jnp.float32), precision=highest)
        mixed = (mixed * (1.0 / math.sqrt(N_SHARD))).astype(jnp.bfloat16).reshape(NBLK, TOK, BLK)
        sketched = jnp.take(mixed, block_ids.reshape(-1), axis=0).reshape(N_SHARD, OWN_BLOCKS, TOK, BLK)
        weighted = jnp.einsum('tu,ojub->ojtb', token_gram.astype(jnp.float32), sketched.astype(jnp.float32), precision=highest).astype(jnp.bfloat16)
        block_gram = jnp.einsum('ojtb,oktc->ojbkc', sketched.astype(jnp.float32), weighted.astype(jnp.float32), precision=highest)
        return (running + block_gram.reshape(N_SHARD * OWN, OWN), None)
    total, unused = lax.scan(accumulate, jnp.zeros((N_SHARD * OWN, OWN), jnp.float32), (seq_acts, seq_grads))
    return total / (N_DP * TOK * D)
```

```python
import functools
import math

import jax
import jax.numpy as jnp
from jax import lax
from jax.experimental import pallas as pl
from jax.experimental.pallas import tpu as pltpu
from jax.sharding import PartitionSpec as P

BLK = 128
CAP = 2


def partner_2(x, axis, distance):
    return lax.ppermute(x, axis, [(i, i ^ 1 << distance) for i in range(lax.axis_size(axis))])


def parity_table(count):
    index = jnp.arange(count, dtype=jnp.int32)
    total = jnp.zeros((count, count), jnp.int32)
    for level in range(count.bit_length() - 1):
        total = total + (
            jnp.right_shift(index[:, None], level) & jnp.right_shift(index[None, :], level) & 1
        )
    return (1 - 2 * (total % 2)).astype(jnp.float32)


def route_sampled(mixed, block_ids, me_index, shards, blocks_per, tokens, width):
    groups = block_ids.shape[1] // CAP
    sources = block_ids[:, ::CAP] // blocks_per
    local_ids = (block_ids % blocks_per).reshape(shards, groups, CAP)
    matched = sources == me_index
    chosen = jnp.sum(jnp.where(matched[:, :, None], local_ids, 0), axis=1)
    live_rows = jnp.any(matched, axis=1).astype(jnp.bfloat16)
    outgoing = jnp.take(mixed, chosen.reshape(-1), axis=0).reshape(shards, CAP, tokens, width)
    return (outgoing * live_rows[:, None, None, None], jnp.take(sources, me_index, axis=0))


def body(activations, out_grads, sign_bits, block_ids):
    shards = lax.axis_size("shard")
    me_index = lax.axis_index("shard")
    tokens = out_grads.shape[0]
    width = BLK
    own_blocks = block_ids.shape[1]
    blocks_per = out_grads.shape[1] // width
    model_width = activations.shape[1] * shards
    inv_block = 1.0 / math.sqrt(width)
    inv_shard = 1.0 / math.sqrt(shards)
    partial_gram = jnp.dot(activations, activations.T, preferred_element_type=jnp.float32)
    token_gram = lax.psum(partial_gram, "shard").astype(jnp.bfloat16)
    sign_values = (1 - 2 * sign_bits).astype(jnp.bfloat16)
    flipped = (out_grads * sign_values[None, :]).reshape(tokens, blocks_per, width)
    block_table = parity_table(width).astype(jnp.bfloat16)
    local_mix = jnp.einsum("tbj,jk->btk", flipped, block_table, preferred_element_type=jnp.float32)
    local_mix = (local_mix * inv_block).astype(jnp.bfloat16)
    running = local_mix.astype(jnp.float32)
    for level in range(shards.bit_length() - 1):
        partner = partner_2(running, "shard", level)
        upper = jnp.right_shift(me_index, level) & 1 == 1
        running = jnp.where(upper, partner - running, running + partner)
    mixed = (running * inv_shard).astype(jnp.bfloat16)
    outgoing, own_sources = route_sampled(
        mixed, block_ids, me_index, shards, blocks_per, tokens, width
    )
    incoming = lax.all_to_all(outgoing, "shard", split_axis=0, concat_axis=0, tiled=True)
    sketched = jnp.take(incoming, own_sources, axis=0).reshape(own_blocks, tokens, width)
    weighted = jnp.einsum(
        "tu,jub->jtb", token_gram, sketched, preferred_element_type=jnp.float32
    ).astype(jnp.bfloat16)
    block_gram = jnp.einsum("jtb,ktc->jbkc", sketched, weighted, preferred_element_type=jnp.float32)
    own_cols = own_blocks * width
    block_gram = block_gram.reshape(own_cols, own_cols)
    summed = lax.psum(block_gram, "dp")
    return summed / (lax.axis_size("dp") * tokens * model_width)


ALONG = pl.DeviceIdType.MESH
CHUNKS = 4
GP = ((0, 0), (256, 256), (256, 0))
FIRST = (0, 1, 3, 6, 10)


def pick_kernel(shards, own, per, ids, bits, grads, out, held, i_sem, o_sem):
    z = lax.axis_index("shard")
    width = BLK
    number = shards * own

    def start_of(p):
        block = ids[p]
        r = block // per
        return r, pl.multiple_of((block - r * per) * width, width)

    def fetch(p):
        return pltpu.make_async_copy(grads.at[:, pl.ds(start_of(p)[1], width)], held.at[p], i_sem.at[p])

    def put(p):
        return pltpu.make_async_copy(held.at[p], out.at[p], o_sem.at[p])

    def first(p, carry):
        fetch(p).start()
        return carry

    def middle(p, carry):
        r, start = start_of(p)
        common = r & z
        odd = common & 1
        for level in range(1, shards.bit_length() - 1):
            odd = odd + ((common >> level) & 1)
        sign = 1 - 2 * (odd & 1)
        signs = ((1 - 2 * bits[:, pl.ds(start, width)]) * sign).astype(jnp.float32).astype(jnp.bfloat16)
        fetch(p).wait()
        held[p] = held[p] * signs
        put(p).start()
        return carry

    def end(p, carry):
        put(p).wait()
        return carry

    lax.fori_loop(0, number, first, 0)
    lax.fori_loop(0, number, middle, 0)
    lax.fori_loop(0, number, end, 0)


def mix_kernel(
    shards, parts, own, act, picked, out,
    rx, tx, grx, gtx, part, full, sketch, halves, prx, rtx, rrx, gathered,
    z_send, z_recv, p_send, p_recv, r_send, r_recv, f_send, f_recv, a_send, a_recv, w_send, w_recv,
):
    z = lax.axis_index("shard")
    d = lax.axis_index("dp")
    core = lax.rem(d, 2)
    chip = d // 2
    last = shards - 1
    edge = (z == 0) | (z == last)
    middle = jnp.logical_not(edge)
    tokens = act.shape[0]
    width = BLK
    inv_block = 1.0 / math.sqrt(width)
    inv_shard = 1.0 / math.sqrt(shards)
    pieces = 2 * own

    barrier = pltpu.get_barrier_semaphore()

    def peer(m):
        flipped = 1 - lax.rem(chip, 2) if m & 1 else lax.rem(chip, 2)
        high = 1 - chip // 2 if m & 2 else chip // 2
        return (high * 2 + flipped) * 2 + core

    partner = chip * 2 + 1 - core
    for m in (1, 2, 3):
        pl.semaphore_signal(barrier, inc=1, device_id={"dp": peer(m)}, device_id_type=ALONG)
    pl.semaphore_signal(barrier, inc=1, device_id={"dp": partner}, device_id_type=ALONG)

    @pl.when(z > 0)
    def _():
        pl.semaphore_signal(barrier, inc=1, device_id={"shard": z - 1}, device_id_type=ALONG)

    @pl.when(z < last)
    def _():
        pl.semaphore_signal(barrier, inc=1, device_id={"shard": z + 1}, device_id_type=ALONG)

    row = lax.broadcasted_iota(jnp.int32, (width, width), 0)
    col = lax.broadcasted_iota(jnp.int32, (width, width), 1)
    both = row & col
    count = both & 1
    for level in range(1, width.bit_length() - 1):
        count = count + ((both >> level) & 1)
    table = (1 - 2 * (count & 1)).astype(jnp.float32).astype(jnp.bfloat16)

    def contribution(owner, j):
        lm = jnp.dot(picked[owner * own + j], table, preferred_element_type=jnp.float32)
        return (lm * inv_block).astype(jnp.bfloat16).astype(jnp.float32) * inv_shard

    def owner_of(way, t):
        return jnp.where(way == 0, 1 - t, 2 + t)

    def target(way):
        return jnp.where(way == 0, z - 1, z + 1)

    def s_copy(way, k):
        return pltpu.make_async_remote_copy(
            tx.at[way, k], rx.at[way, k], z_send.at[way, 3 + k], z_recv.at[way, 3 + k],
            device_id={"shard": target(way)}, device_id_type=ALONG)

    def g_copy(way, i):
        return pltpu.make_async_remote_copy(
            gtx.at[way, i], grx.at[way, i], z_send.at[way, i], z_recv.at[way, i],
            device_id={"shard": target(way)}, device_id_type=ALONG)

    def gpart(i):
        r0, c0 = GP[i]
        return part[r0 : r0 + 256, c0 : c0 + 256]

    def ids_of(k):
        return k // own, k % own

    def units(c):
        return pl.ds(FIRST[c], c + 1)

    def a_copy(c, slot, who):
        return pltpu.make_async_remote_copy(
            gathered.at[d, units(c)], gathered.at[d, units(c)], a_send.at[c, slot], a_recv.at[c, slot],
            device_id={"dp": who}, device_id_type=ALONG)

    def a_recv_from(c, slot, who):
        return pltpu.make_async_remote_copy(
            gathered.at[who, units(c)], gathered.at[who, units(c)], a_send.at[c, slot], a_recv.at[c, slot],
            device_id={"dp": who}, device_id_type=ALONG)

    def w_copy(c, m):
        return pltpu.make_async_remote_copy(
            gathered.at[peer(m), units(c)], gathered.at[peer(m), units(c)],
            w_send.at[c, m - 1], w_recv.at[c, m - 1],
            device_id={"dp": partner}, device_id_type=ALONG)

    def w_recv_from(c, m):
        other = peer(m) + 1 - 2 * core
        return pltpu.make_async_remote_copy(
            gathered.at[other, units(c)], gathered.at[other, units(c)],
            w_send.at[c, m - 1], w_recv.at[c, m - 1],
            device_id={"dp": partner}, device_id_type=ALONG)

    def spread(c):
        for m in (1, 2, 3):
            a_copy(c, m - 1, peer(m)).start()
        a_copy(c, 3, partner).start()

    def relay(c):
        for m in (1, 2, 3):
            a_recv_from(c, m - 1, peer(m)).wait_recv()
            w_copy(c, m).start()

    def settle(c):
        a_recv_from(c, 3, partner).wait_recv()
        for m in (1, 2, 3):
            w_recv_from(c, m).wait_recv()
        for m in (1, 2, 3):
            a_copy(c, m - 1, peer(m)).wait_send()
            w_copy(c, m).wait_send()
        a_copy(c, 3, partner).wait_send()

    def f_copy(c):
        inward = jnp.where(z == 0, 1, last - 1)
        return pltpu.make_async_remote_copy(
            rrx.at[3, units(c)], gathered.at[d, units(c)], f_send.at[c], f_recv.at[c],
            device_id={"shard": inward}, device_id_type=ALONG)

    def f_recv_at():
        def make(c):
            outward = jnp.where(z == 1, 0, last)
            return pltpu.make_async_remote_copy(
                rrx.at[3, units(c)], gathered.at[d, units(c)], f_send.at[c], f_recv.at[c],
                device_id={"shard": outward}, device_id_type=ALONG)
        return make

    part[...] = lax.dot_general(act[...], act[...], (((1,), (1,)), ((), ())), preferred_element_type=jnp.float32)

    @pl.when(edge)
    def _():
        pl.semaphore_wait(barrier, 5)

    @pl.when(middle)
    def _():
        pl.semaphore_wait(barrier, 6)

    @pl.when(edge)
    def _():
        out_way = jnp.where(z == 0, 1, 0)
        in_way = 1 - out_way
        for i in range(3):
            gtx[out_way, i] = gpart(i).astype(jnp.bfloat16)
            g_copy(out_way, i).start()

        def push(k, carry):
            t, j = k // own, lax.rem(k, own)
            tx[out_way, k] = contribution(owner_of(out_way, t), j).astype(jnp.bfloat16)
            s_copy(out_way, k).start()
            return carry

        lax.fori_loop(0, pieces, push, 0)

        for i in range(3):
            r0, c0 = GP[i]
            pltpu.make_async_remote_copy(
                gtx.at[in_way, i], grx.at[in_way, i], z_send.at[in_way, i], z_recv.at[in_way, i],
                device_id={"shard": target(out_way)}, device_id_type=ALONG).wait_recv()
            block = (grx[in_way, i].astype(jnp.float32) + gpart(i)).astype(jnp.bfloat16)
            full[r0 : r0 + 256, c0 : c0 + 256] = block
            if r0 != c0:
                full[c0 : c0 + 256, r0 : r0 + 256] = block.T

        def where(q):
            t, c = q // CHUNKS, q % CHUNKS
            return t, c, pl.ds(10 * t + FIRST[c], c + 1)

        def p_copy(q):
            t, c, us = where(q)
            return pltpu.make_async_remote_copy(
                halves.at[1 - core, us], prx.at[us], p_send.at[q], p_recv.at[q],
                device_id={"dp": partner}, device_id_type=ALONG)

        def r_copy(q, m):
            t, c, us = where(q)
            return pltpu.make_async_remote_copy(
                rtx.at[peer(m) // 2, us], rrx.at[m - 1, us], r_send.at[q, m - 1], r_recv.at[q, m - 1],
                device_id={"dp": peer(m)}, device_id_type=ALONG)

        def step_a(q):
            t, c, us = where(q)
            for side in range(2):
                j = 2 * c + side
                k = own * t + j
                mine = contribution(owner_of(in_way, t), j)
                pltpu.make_async_remote_copy(
                    tx.at[in_way, k], rx.at[in_way, k], z_send.at[in_way, 3 + k], z_recv.at[in_way, 3 + k],
                    device_id={"shard": target(out_way)}, device_id_type=ALONG).wait_recv()
                done = (rx[in_way, k].astype(jnp.float32) + mine).astype(jnp.bfloat16)
                sketch[t, :, width * j : width * (j + 1)] = done
            cols = sketch[t, :, 256 * c : 256 * (c + 1)]
            weighted = jnp.dot(full[...], cols, preferred_element_type=jnp.float32).astype(jnp.bfloat16)
            for i in range(c + 1):
                unit = lax.dot_general(
                    sketch[t, :, 256 * i : 256 * (i + 1)], weighted, (((0,), (0,)), ((), ())),
                    preferred_element_type=jnp.float32)
                halves[0, 10 * t + FIRST[c] + i] = unit[:128]
                halves[1, 10 * t + FIRST[c] + i] = unit[128:]
            p_copy(q).start()

        def step_b(q):
            t, c, us = where(q)
            p_copy(q).wait_recv()
            for i in range(c + 1):
                u = 10 * t + FIRST[c] + i
                total = (halves[core, u] + prx[u]).astype(jnp.bfloat16)
                for n in range(4):
                    rtx[n, u] = total[32 * n : 32 * (n + 1)]
            for m in (1, 2, 3):
                r_copy(q, m).start()

        def step_c(q):
            t, c, us = where(q)
            for m in (1, 2, 3):
                r_copy(q, m).wait_recv()
            for i in range(c + 1):
                u = 10 * t + FIRST[c] + i
                total = rtx[chip, u].astype(jnp.float32)
                for m in range(3):
                    total = total + rrx[m, u].astype(jnp.float32)
                total = (total * (1.0 / (parts * tokens * act.shape[1] * shards))).astype(jnp.bfloat16)
                if t == 0:
                    rrx[3, FIRST[c] + i] = total
                else:
                    gathered[d, FIRST[c] + i] = total
            if t == 0:
                f_copy(c).start()
            else:
                spread(c)

        def step_d(q):
            if q >= CHUNKS:
                relay(q - CHUNKS)

        steps = 2 * CHUNKS
        for q in range(steps + 3):
            if 0 <= q - 1 < steps:
                step_b(q - 1)
            if 0 <= q - 2 < steps:
                step_c(q - 2)
            if 0 <= q - 3 < steps:
                step_d(q - 3)
            if q < steps:
                step_a(q)
        for c in range(CHUNKS):
            settle(c)
            f_copy(c).wait_send()
        for q in range(steps):
            p_copy(q).wait_send()
            for m in (1, 2, 3):
                r_copy(q, m).wait_send()
        for i in range(3):
            g_copy(out_way, i).wait_send()

        def drain(k, carry):
            s_copy(out_way, k).wait_send()
            return carry

        lax.fori_loop(0, pieces, drain, 0)

    @pl.when(middle)
    def _():
        near = jnp.where(z == 1, 1, 0)
        far = 1 - near

        def pass_g(way, i):
            g_copy(way, i).wait_recv()
            gtx[way, i] = (grx[way, i].astype(jnp.float32) + gpart(i)).astype(jnp.bfloat16)
            g_copy(way, i).start()

        def pass_s(way, k):
            t, j = k // own, lax.rem(k, own)
            mine = contribution(owner_of(way, t), j)
            s_copy(way, k).wait_recv()
            tx[way, k] = (rx[way, k].astype(jnp.float32) + mine).astype(jnp.bfloat16)
            s_copy(way, k).start()

        pass_g(near, 0)
        pass_g(near, 1)
        pass_g(far, 0)
        pass_g(near, 2)
        pass_g(far, 1)
        pass_s(near, 0)
        pass_g(far, 2)

        def both_ways(k, carry):
            pass_s(near, k)
            pass_s(far, k - 1)
            return carry

        lax.fori_loop(1, pieces, both_ways, 0)
        pass_s(far, pieces - 1)
        arrival = f_recv_at()
        for c in range(CHUNKS):
            arrival(c).wait_recv()
            spread(c)
        for c in range(CHUNKS):
            relay(c)
        for c in range(CHUNKS):
            settle(c)
        for way in range(2):
            for i in range(3):
                g_copy(way, i).wait_send()

        def drain(k, carry):
            s_copy(0, k).wait_send()
            s_copy(1, k).wait_send()
            return carry

        lax.fori_loop(0, pieces, drain, 0)

    out[...] = gathered[...]


def assemble_kernel(got, out):
    for c in range(CHUNKS):
        for i in range(c + 1):
            u = FIRST[c] + i
            rows = [got[2 * n + h, u] for h in range(2) for n in range(4)]
            unit = jnp.concatenate(rows, axis=0).astype(jnp.float32)
            out[256 * i : 256 * (i + 1), 256 * c : 256 * (c + 1)] = unit
            if i != c:
                out[256 * c : 256 * (c + 1), 256 * i : 256 * (i + 1)] = unit.T


def fast_body(shards, parts, activations, out_grads, sign_bits, block_ids):
    tokens, columns = out_grads.shape
    per = columns // BLK
    own = block_ids.shape[1]
    vmem = pl.BlockSpec(memory_space=pltpu.VMEM)
    bf, f32 = jnp.bfloat16, jnp.float32
    dma = pltpu.SemaphoreType.DMA
    number = shards * own
    picked = pl.pallas_call(
        functools.partial(pick_kernel, shards, own, per),
        out_shape=jax.ShapeDtypeStruct((number, tokens, BLK), bf),
        in_specs=[pl.BlockSpec(memory_space=pltpu.SMEM), vmem, pl.BlockSpec(memory_space=pl.ANY)],
        out_specs=pl.BlockSpec(memory_space=pl.ANY),
        scratch_shapes=[pltpu.VMEM((number, tokens, BLK), bf), dma((number,)), dma((number,))],
        name="pick",
    )(block_ids.reshape(-1), sign_bits.reshape(1, columns), out_grads)
    got = pl.pallas_call(
        functools.partial(mix_kernel, shards, parts, own),
        out_shape=jax.ShapeDtypeStruct((parts, 10, 32, 256), bf),
        in_specs=[vmem, vmem],
        out_specs=vmem,
        scratch_shapes=[
            pltpu.VMEM((2, 2 * own, tokens, BLK), bf),
            pltpu.VMEM((2, 2 * own, tokens, BLK), bf),
            pltpu.VMEM((2, 3, 256, 256), bf),
            pltpu.VMEM((2, 3, 256, 256), bf),
            pltpu.VMEM((tokens, tokens), f32),
            pltpu.VMEM((tokens, tokens), bf),
            pltpu.VMEM((2, tokens, own * BLK), bf),
            pltpu.VMEM((2, 20, 128, 256), f32),
            pltpu.VMEM((20, 128, 256), f32),
            pltpu.VMEM((4, 20, 32, 256), bf),
            pltpu.VMEM((4, 20, 32, 256), bf),
            pltpu.VMEM((parts, 10, 32, 256), bf),
            dma((2, 3 + 2 * own)), dma((2, 3 + 2 * own)),
            dma((8,)), dma((8,)),
            dma((8, 3)), dma((8, 3)),
            dma((4,)), dma((4,)),
            dma((4, 4)), dma((4, 4)),
            dma((4, 3)), dma((4, 3)),
        ],
        compiler_params=pltpu.CompilerParams(collective_id=0, has_side_effects=True, vmem_limit_bytes=56 * 2**20),
        name="mix",
    )(activations, picked)
    return pl.pallas_call(
        assemble_kernel,
        out_shape=jax.ShapeDtypeStruct((own * BLK, own * BLK), f32),
        in_specs=[vmem],
        out_specs=vmem,
        name="assemble",
    )(got)


def solution(mesh):
    in_specs = (P("dp", "shard"), P("dp", "shard"), P("shard"), P())
    out_specs = P("shard", None)
    shards, parts = mesh.shape["shard"], mesh.shape["dp"]
    chosen = functools.partial(fast_body, shards, parts) if (shards, parts) == (4, 8) else body
    return jax.shard_map(chosen, mesh=mesh, in_specs=in_specs, out_specs=out_specs, check_vma=False)
```

```python
import functools
import math

import jax
import jax.numpy as jnp
from jax import lax
from jax.experimental import pallas as pl
from jax.experimental.pallas import tpu as pltpu
from jax.sharding import PartitionSpec as P

BLK = 128
CAP = 2


def partner_2(x, axis, distance):
    return lax.ppermute(x, axis, [(i, i ^ 1 << distance) for i in range(lax.axis_size(axis))])


def parity_table(count):
    index = jnp.arange(count, dtype=jnp.int32)
    total = jnp.zeros((count, count), jnp.int32)
    for level in range(count.bit_length() - 1):
        total = total + (
            jnp.right_shift(index[:, None], level) & jnp.right_shift(index[None, :], level) & 1
        )
    return (1 - 2 * (total % 2)).astype(jnp.float32)


def route_sampled(mixed, block_ids, me_index, shards, blocks_per, tokens, width):
    groups = block_ids.shape[1] // CAP
    sources = block_ids[:, ::CAP] // blocks_per
    local_ids = (block_ids % blocks_per).reshape(shards, groups, CAP)
    matched = sources == me_index
    chosen = jnp.sum(jnp.where(matched[:, :, None], local_ids, 0), axis=1)
    live_rows = jnp.any(matched, axis=1).astype(jnp.bfloat16)
    outgoing = jnp.take(mixed, chosen.reshape(-1), axis=0).reshape(shards, CAP, tokens, width)
    return (outgoing * live_rows[:, None, None, None], jnp.take(sources, me_index, axis=0))


def body(activations, out_grads, sign_bits, block_ids):
    shards = lax.axis_size("shard")
    me_index = lax.axis_index("shard")
    tokens = out_grads.shape[0]
    width = BLK
    own_blocks = block_ids.shape[1]
    blocks_per = out_grads.shape[1] // width
    model_width = activations.shape[1] * shards
    inv_block = 1.0 / math.sqrt(width)
    inv_shard = 1.0 / math.sqrt(shards)
    partial_gram = jnp.dot(activations, activations.T, preferred_element_type=jnp.float32)
    token_gram = lax.psum(partial_gram, "shard").astype(jnp.bfloat16)
    sign_values = (1 - 2 * sign_bits).astype(jnp.bfloat16)
    flipped = (out_grads * sign_values[None, :]).reshape(tokens, blocks_per, width)
    block_table = parity_table(width).astype(jnp.bfloat16)
    local_mix = jnp.einsum("tbj,jk->btk", flipped, block_table, preferred_element_type=jnp.float32)
    local_mix = (local_mix * inv_block).astype(jnp.bfloat16)
    running = local_mix.astype(jnp.float32)
    for level in range(shards.bit_length() - 1):
        partner = partner_2(running, "shard", level)
        upper = jnp.right_shift(me_index, level) & 1 == 1
        running = jnp.where(upper, partner - running, running + partner)
    mixed = (running * inv_shard).astype(jnp.bfloat16)
    outgoing, own_sources = route_sampled(
        mixed, block_ids, me_index, shards, blocks_per, tokens, width
    )
    incoming = lax.all_to_all(outgoing, "shard", split_axis=0, concat_axis=0, tiled=True)
    sketched = jnp.take(incoming, own_sources, axis=0).reshape(own_blocks, tokens, width)
    weighted = jnp.einsum(
        "tu,jub->jtb", token_gram, sketched, preferred_element_type=jnp.float32
    ).astype(jnp.bfloat16)
    block_gram = jnp.einsum("jtb,ktc->jbkc", sketched, weighted, preferred_element_type=jnp.float32)
    own_cols = own_blocks * width
    block_gram = block_gram.reshape(own_cols, own_cols)
    summed = lax.psum(block_gram, "dp")
    return summed / (lax.axis_size("dp") * tokens * model_width)


ALONG = pl.DeviceIdType.MESH
SPANS = ((0, 2), (2, 4), (4, 6), (6, 7), (7, 8))
CHUNKS = len(SPANS)
FIRST = tuple(sum((hi - lo) * hi for lo, hi in SPANS[:c]) for c in range(CHUNKS + 1))
UNITS = FIRST[CHUNKS]
TRIANGLE = tuple((i, j) for i in range(4) for j in range(i + 1))
GSPANS = ((0, 4), (4, 7), (7, 10))


def pick_kernel(shards, own, per, ids, bits, grads, out):
    z = lax.axis_index("shard")
    width = BLK
    number = shards * own

    def start_of(p):
        block = ids[p // own, lax.rem(p, own)]
        r = block // per
        return r, pl.multiple_of((block - r * per) * width, width)

    def take(p, carry):
        r, start = start_of(p)
        common = r & z
        odd = common & 1
        for level in range(1, shards.bit_length() - 1):
            odd = odd + ((common >> level) & 1)
        sign = 1 - 2 * (odd & 1)
        signs = ((1 - 2 * bits[pl.ds(start, width)].reshape(1, width)) * sign).astype(jnp.float32).astype(jnp.bfloat16)
        out[p] = grads[:, pl.ds(start, width)] * signs
        return carry

    lax.fori_loop(0, number, take, 0)


def mix_kernel(
    shards, parts, own, act, picked, out,
    rx, tx, grx, gtx, part, full, sketch, halves, prx, rtx, rrx, gathered,
    z_send, z_recv, p_send, p_recv, r_send, r_recv, f_send, f_recv, a_send, a_recv, w_send, w_recv,
):
    z = lax.axis_index("shard")
    d = lax.axis_index("dp")
    core = lax.rem(d, 2)
    chip = d // 2
    last = shards - 1
    edge = (z == 0) | (z == last)
    middle = jnp.logical_not(edge)
    tokens = act.shape[0]
    width = BLK
    inv_block = 1.0 / math.sqrt(width)
    inv_shard = 1.0 / math.sqrt(shards)
    pieces = 2 * own

    barrier = pltpu.get_barrier_semaphore()

    def peer(m):
        flipped = 1 - lax.rem(chip, 2) if m & 1 else lax.rem(chip, 2)
        high = 1 - chip // 2 if m & 2 else chip // 2
        return (high * 2 + flipped) * 2 + core

    partner = chip * 2 + 1 - core
    for m in (1, 2, 3):
        pl.semaphore_signal(barrier, inc=1, device_id={"dp": peer(m)}, device_id_type=ALONG)
    pl.semaphore_signal(barrier, inc=1, device_id={"dp": partner}, device_id_type=ALONG)

    @pl.when(z > 0)
    def _():
        pl.semaphore_signal(barrier, inc=1, device_id={"shard": z - 1}, device_id_type=ALONG)

    @pl.when(z < last)
    def _():
        pl.semaphore_signal(barrier, inc=1, device_id={"shard": z + 1}, device_id_type=ALONG)

    row = lax.broadcasted_iota(jnp.int32, (width, width), 0)
    col = lax.broadcasted_iota(jnp.int32, (width, width), 1)
    both = row & col
    count = both & 1
    for level in range(1, width.bit_length() - 1):
        count = count + ((both >> level) & 1)
    table = (1 - 2 * (count & 1)).astype(jnp.float32).astype(jnp.bfloat16)

    def contribution(owner, j):
        lm = jnp.dot(picked[owner * own + j], table, preferred_element_type=jnp.float32)
        return (lm * inv_block).astype(jnp.bfloat16).astype(jnp.float32) * inv_shard

    def owner_of(way, t):
        return jnp.where(way == 0, 1 - t, 2 + t)

    def target(way):
        return jnp.where(way == 0, z - 1, z + 1)

    def s_copy(way, k):
        return pltpu.make_async_remote_copy(
            tx.at[way, k], rx.at[way, k], z_send.at[way, 3 + k], z_recv.at[way, 3 + k],
            device_id={"shard": target(way)}, device_id_type=ALONG)

    def g_copy(way, i):
        lo, hi = GSPANS[i]
        return pltpu.make_async_remote_copy(
            gtx.at[way, lo:hi], grx.at[way, lo:hi], z_send.at[way, i], z_recv.at[way, i],
            device_id={"shard": target(way)}, device_id_type=ALONG)

    def gpart(n):
        i, j = TRIANGLE[n]
        return part[128 * i : 128 * (i + 1), 128 * j : 128 * (j + 1)]

    def units(c):
        return pl.ds(FIRST[c], FIRST[c + 1] - FIRST[c])

    def a_copy(c, slot, who):
        return pltpu.make_async_remote_copy(
            gathered.at[d, units(c)], gathered.at[d, units(c)], a_send.at[c, slot], a_recv.at[c, slot],
            device_id={"dp": who}, device_id_type=ALONG)

    def a_recv_from(c, slot, who):
        return pltpu.make_async_remote_copy(
            gathered.at[who, units(c)], gathered.at[who, units(c)], a_send.at[c, slot], a_recv.at[c, slot],
            device_id={"dp": who}, device_id_type=ALONG)

    def w_copy(c, m):
        return pltpu.make_async_remote_copy(
            gathered.at[peer(m), units(c)], gathered.at[peer(m), units(c)],
            w_send.at[c, m - 1], w_recv.at[c, m - 1],
            device_id={"dp": partner}, device_id_type=ALONG)

    def w_recv_from(c, m):
        other = peer(m) + 1 - 2 * core
        return pltpu.make_async_remote_copy(
            gathered.at[other, units(c)], gathered.at[other, units(c)],
            w_send.at[c, m - 1], w_recv.at[c, m - 1],
            device_id={"dp": partner}, device_id_type=ALONG)

    def spread(c):
        for m in (1, 2, 3):
            a_copy(c, m - 1, peer(m)).start()
        a_copy(c, 3, partner).start()

    def relay(c):
        for m in (1, 2, 3):
            a_recv_from(c, m - 1, peer(m)).wait_recv()
            w_copy(c, m).start()

    def settle(c):
        a_recv_from(c, 3, partner).wait_recv()
        for m in (1, 2, 3):
            w_recv_from(c, m).wait_recv()
        for m in (1, 2, 3):
            a_copy(c, m - 1, peer(m)).wait_send()
            w_copy(c, m).wait_send()
        a_copy(c, 3, partner).wait_send()

    def f_copy(c):
        inward = jnp.where(z == 0, 1, last - 1)
        return pltpu.make_async_remote_copy(
            rrx.at[3, units(c)], gathered.at[d, units(c)], f_send.at[c], f_recv.at[c],
            device_id={"shard": inward}, device_id_type=ALONG)

    def f_recv_at():
        def make(c):
            outward = jnp.where(z == 1, 0, last)
            return pltpu.make_async_remote_copy(
                rrx.at[3, units(c)], gathered.at[d, units(c)], f_send.at[c], f_recv.at[c],
                device_id={"shard": outward}, device_id_type=ALONG)
        return make

    part[...] = lax.dot_general(act[...], act[...], (((1,), (1,)), ((), ())), preferred_element_type=jnp.float32)

    @pl.when(edge)
    def _():
        pl.semaphore_wait(barrier, 5)

    @pl.when(middle)
    def _():
        pl.semaphore_wait(barrier, 6)

    @pl.when(edge)
    def _():
        out_way = jnp.where(z == 0, 1, 0)
        in_way = 1 - out_way
        for i in range(3):
            for n in range(*GSPANS[i]):
                gtx[out_way, n] = gpart(n).astype(jnp.bfloat16)
            g_copy(out_way, i).start()

        def push(k, carry):
            t, j = k // own, lax.rem(k, own)
            tx[out_way, k] = contribution(owner_of(out_way, t), j).astype(jnp.bfloat16)
            s_copy(out_way, k).start()
            return carry

        lax.fori_loop(0, pieces, push, 0)

        for i in range(3):
            lo, hi = GSPANS[i]
            pltpu.make_async_remote_copy(
                gtx.at[in_way, lo:hi], grx.at[in_way, lo:hi], z_send.at[in_way, i], z_recv.at[in_way, i],
                device_id={"shard": target(out_way)}, device_id_type=ALONG).wait_recv()
            for n in range(lo, hi):
                r, c = TRIANGLE[n]
                block = (grx[in_way, n].astype(jnp.float32) + gpart(n)).astype(jnp.bfloat16)
                full[128 * r : 128 * (r + 1), 128 * c : 128 * (c + 1)] = block
                if r != c:
                    full[128 * c : 128 * (c + 1), 128 * r : 128 * (r + 1)] = block.T

        def where(q):
            t, c = q // CHUNKS, q % CHUNKS
            return t, c, pl.ds(UNITS * t + FIRST[c], FIRST[c + 1] - FIRST[c])

        def p_copy(q):
            t, c, us = where(q)
            return pltpu.make_async_remote_copy(
                halves.at[1 - core, us], prx.at[us], p_send.at[q], p_recv.at[q],
                device_id={"dp": partner}, device_id_type=ALONG)

        def r_copy(q, m):
            t, c, us = where(q)
            return pltpu.make_async_remote_copy(
                rtx.at[peer(m) // 2, us], rrx.at[m - 1, us], r_send.at[q, m - 1], r_recv.at[q, m - 1],
                device_id={"dp": peer(m)}, device_id_type=ALONG)

        def step_a(q):
            t, c, us = where(q)
            lo, hi = SPANS[c]
            for j in range(lo, hi):
                k = own * t + j
                mine = contribution(owner_of(in_way, t), j)
                pltpu.make_async_remote_copy(
                    tx.at[in_way, k], rx.at[in_way, k], z_send.at[in_way, 3 + k], z_recv.at[in_way, 3 + k],
                    device_id={"shard": target(out_way)}, device_id_type=ALONG).wait_recv()
                done = (rx[in_way, k].astype(jnp.float32) + mine).astype(jnp.bfloat16)
                sketch[t, :, width * j : width * (j + 1)] = done
            cols = sketch[t, :, width * lo : width * hi]
            weighted = jnp.dot(full[...], cols, preferred_element_type=jnp.float32).astype(jnp.bfloat16)
            for top in range(0, hi, 2):
                end = min(top + 2, hi)
                unit = lax.dot_general(
                    sketch[t, :, width * top : width * end], weighted, (((0,), (0,)), ((), ())),
                    preferred_element_type=jnp.float32)
                for i in range(top, end):
                    for j in range(lo, hi):
                        u = UNITS * t + FIRST[c] + (j - lo) * hi + i
                        block = unit[128 * (i - top) : 128 * (i - top + 1), width * (j - lo) : width * (j - lo + 1)]
                        halves[0, u] = block[:64]
                        halves[1, u] = block[64:]
            p_copy(q).start()

        def step_b(q):
            t, c, us = where(q)
            p_copy(q).wait_recv()
            total = (halves[core, us] + prx[us]).astype(jnp.bfloat16)
            for n in range(4):
                rtx[n, us] = total[:, 16 * n : 16 * (n + 1)]
            for m in (1, 2, 3):
                r_copy(q, m).start()

        def step_c(q):
            t, c, us = where(q)
            for m in (1, 2, 3):
                r_copy(q, m).wait_recv()
            total = rtx[chip, us].astype(jnp.float32)
            for m in range(3):
                total = total + rrx[m, us].astype(jnp.float32)
            total = (total * (1.0 / (parts * tokens * act.shape[1] * shards))).astype(jnp.bfloat16)
            if t == 0:
                rrx[3, units(c)] = total
            else:
                gathered[d, units(c)] = total
            if t == 0:
                f_copy(c).start()
            else:
                spread(c)

        def step_d(q):
            if q >= CHUNKS:
                relay(q - CHUNKS)

        steps = 2 * CHUNKS
        for q in range(steps + 3):
            if 0 <= q - 1 < steps:
                step_b(q - 1)
            if 0 <= q - 2 < steps:
                step_c(q - 2)
            if 0 <= q - 3 < steps:
                step_d(q - 3)
            if q < steps:
                step_a(q)
        for c in range(CHUNKS):
            settle(c)
            f_copy(c).wait_send()
        for q in range(steps):
            p_copy(q).wait_send()
            for m in (1, 2, 3):
                r_copy(q, m).wait_send()
        for i in range(3):
            g_copy(out_way, i).wait_send()

        def drain(k, carry):
            s_copy(out_way, k).wait_send()
            return carry

        lax.fori_loop(0, pieces, drain, 0)

    @pl.when(middle)
    def _():
        near = jnp.where(z == 1, 1, 0)
        far = 1 - near

        def pass_g(way, i):
            g_copy(way, i).wait_recv()
            for n in range(*GSPANS[i]):
                gtx[way, n] = (grx[way, n].astype(jnp.float32) + gpart(n)).astype(jnp.bfloat16)
            g_copy(way, i).start()

        def pass_s(way, k):
            t, j = k // own, lax.rem(k, own)
            mine = contribution(owner_of(way, t), j)
            s_copy(way, k).wait_recv()
            tx[way, k] = (rx[way, k].astype(jnp.float32) + mine).astype(jnp.bfloat16)
            s_copy(way, k).start()

        pass_g(near, 0)
        pass_g(near, 1)
        pass_g(far, 0)
        pass_g(near, 2)
        pass_g(far, 1)
        pass_s(near, 0)
        pass_g(far, 2)

        def both_ways(k, carry):
            pass_s(near, k)
            pass_s(far, k - 1)
            return carry

        lax.fori_loop(1, pieces, both_ways, 0)
        pass_s(far, pieces - 1)
        arrival = f_recv_at()
        for c in range(CHUNKS):
            arrival(c).wait_recv()
            spread(c)
        for c in range(CHUNKS):
            relay(c)
        for c in range(CHUNKS):
            settle(c)
        for way in range(2):
            for i in range(3):
                g_copy(way, i).wait_send()

        def drain(k, carry):
            s_copy(0, k).wait_send()
            s_copy(1, k).wait_send()
            return carry

        lax.fori_loop(0, pieces, drain, 0)

    out[...] = gathered[...]


def assemble_kernel(got, out):
    for c, (lo, hi) in enumerate(SPANS):
        for j in range(lo, hi):
            for i in range(hi):
                u = FIRST[c] + (j - lo) * hi + i
                rows = [got[2 * n + h, u] for h in range(2) for n in range(4)]
                unit = jnp.concatenate(rows, axis=0).astype(jnp.float32)
                out[128 * i : 128 * (i + 1), 128 * j : 128 * (j + 1)] = unit
                if i < lo:
                    out[128 * j : 128 * (j + 1), 128 * i : 128 * (i + 1)] = unit.T


def fast_body(shards, parts, activations, out_grads, sign_bits, block_ids):
    tokens, columns = out_grads.shape
    per = columns // BLK
    own = block_ids.shape[1]
    vmem = pl.BlockSpec(memory_space=pltpu.VMEM)
    bf, f32 = jnp.bfloat16, jnp.float32
    dma = pltpu.SemaphoreType.DMA
    number = shards * own
    picked = pl.pallas_call(
        functools.partial(pick_kernel, shards, own, per),
        out_shape=jax.ShapeDtypeStruct((number, tokens, BLK), bf),
        in_specs=[pl.BlockSpec(memory_space=pltpu.SMEM), vmem, vmem],
        out_specs=vmem,
        compiler_params=pltpu.CompilerParams(vmem_limit_bytes=12 * 2**20),
        name="pick",
    )(block_ids, sign_bits, out_grads)
    got = pl.pallas_call(
        functools.partial(mix_kernel, shards, parts, own),
        out_shape=jax.ShapeDtypeStruct((parts, UNITS, 16, BLK), bf),
        in_specs=[vmem, vmem],
        out_specs=vmem,
        scratch_shapes=[
            pltpu.VMEM((2, 2 * own, tokens, BLK), bf),
            pltpu.VMEM((2, 2 * own, tokens, BLK), bf),
            pltpu.VMEM((2, 10, 128, 128), bf),
            pltpu.VMEM((2, 10, 128, 128), bf),
            pltpu.VMEM((tokens, tokens), f32),
            pltpu.VMEM((tokens, tokens), bf),
            pltpu.VMEM((2, tokens, own * BLK), bf),
            pltpu.VMEM((2, 2 * UNITS, 64, BLK), f32),
            pltpu.VMEM((2 * UNITS, 64, BLK), f32),
            pltpu.VMEM((4, 2 * UNITS, 16, BLK), bf),
            pltpu.VMEM((4, 2 * UNITS, 16, BLK), bf),
            pltpu.VMEM((parts, UNITS, 16, BLK), bf),
            dma((2, 3 + 2 * own)), dma((2, 3 + 2 * own)),
            dma((2 * CHUNKS,)), dma((2 * CHUNKS,)),
            dma((2 * CHUNKS, 3)), dma((2 * CHUNKS, 3)),
            dma((CHUNKS,)), dma((CHUNKS,)),
            dma((CHUNKS, 4)), dma((CHUNKS, 4)),
            dma((CHUNKS, 3)), dma((CHUNKS, 3)),
        ],
        compiler_params=pltpu.CompilerParams(collective_id=0, has_side_effects=True, vmem_limit_bytes=40 * 2**20),
        name="mix",
    )(activations, picked)
    return pl.pallas_call(
        assemble_kernel,
        out_shape=jax.ShapeDtypeStruct((own * BLK, own * BLK), f32),
        in_specs=[vmem],
        out_specs=vmem,
        compiler_params=pltpu.CompilerParams(vmem_limit_bytes=16 * 2**20),
        name="assemble",
    )(got)


def solution(mesh):
    in_specs = (P("dp", "shard"), P("dp", "shard"), P("shard"), P())
    out_specs = P("shard", None)
    shards, parts = mesh.shape["shard"], mesh.shape["dp"]
    chosen = functools.partial(fast_body, shards, parts) if (shards, parts) == (4, 8) else body
    return jax.shard_map(chosen, mesh=mesh, in_specs=in_specs, out_specs=out_specs, check_vma=False)
```

```python
import functools
import math

import jax
import jax.numpy as jnp
from jax import lax
from jax.experimental import pallas as pl
from jax.experimental.pallas import tpu as pltpu
from jax.sharding import PartitionSpec as P

BLK = 128
CAP = 2


def partner_2(x, axis, distance):
    return lax.ppermute(x, axis, [(i, i ^ 1 << distance) for i in range(lax.axis_size(axis))])


def parity_table(count):
    index = jnp.arange(count, dtype=jnp.int32)
    total = jnp.zeros((count, count), jnp.int32)
    for level in range(count.bit_length() - 1):
        total = total + (
            jnp.right_shift(index[:, None], level) & jnp.right_shift(index[None, :], level) & 1
        )
    return (1 - 2 * (total % 2)).astype(jnp.float32)


def route_sampled(mixed, block_ids, me_index, shards, blocks_per, tokens, width):
    groups = block_ids.shape[1] // CAP
    sources = block_ids[:, ::CAP] // blocks_per
    local_ids = (block_ids % blocks_per).reshape(shards, groups, CAP)
    matched = sources == me_index
    chosen = jnp.sum(jnp.where(matched[:, :, None], local_ids, 0), axis=1)
    live_rows = jnp.any(matched, axis=1).astype(jnp.bfloat16)
    outgoing = jnp.take(mixed, chosen.reshape(-1), axis=0).reshape(shards, CAP, tokens, width)
    return (outgoing * live_rows[:, None, None, None], jnp.take(sources, me_index, axis=0))


def body(activations, out_grads, sign_bits, block_ids):
    shards = lax.axis_size("shard")
    me_index = lax.axis_index("shard")
    tokens = out_grads.shape[0]
    width = BLK
    own_blocks = block_ids.shape[1]
    blocks_per = out_grads.shape[1] // width
    model_width = activations.shape[1] * shards
    inv_block = 1.0 / math.sqrt(width)
    inv_shard = 1.0 / math.sqrt(shards)
    partial_gram = jnp.dot(activations, activations.T, preferred_element_type=jnp.float32)
    token_gram = lax.psum(partial_gram, "shard").astype(jnp.bfloat16)
    sign_values = (1 - 2 * sign_bits).astype(jnp.bfloat16)
    flipped = (out_grads * sign_values[None, :]).reshape(tokens, blocks_per, width)
    block_table = parity_table(width).astype(jnp.bfloat16)
    local_mix = jnp.einsum("tbj,jk->btk", flipped, block_table, preferred_element_type=jnp.float32)
    local_mix = (local_mix * inv_block).astype(jnp.bfloat16)
    running = local_mix.astype(jnp.float32)
    for level in range(shards.bit_length() - 1):
        partner = partner_2(running, "shard", level)
        upper = jnp.right_shift(me_index, level) & 1 == 1
        running = jnp.where(upper, partner - running, running + partner)
    mixed = (running * inv_shard).astype(jnp.bfloat16)
    outgoing, own_sources = route_sampled(
        mixed, block_ids, me_index, shards, blocks_per, tokens, width
    )
    incoming = lax.all_to_all(outgoing, "shard", split_axis=0, concat_axis=0, tiled=True)
    sketched = jnp.take(incoming, own_sources, axis=0).reshape(own_blocks, tokens, width)
    weighted = jnp.einsum(
        "tu,jub->jtb", token_gram, sketched, preferred_element_type=jnp.float32
    ).astype(jnp.bfloat16)
    block_gram = jnp.einsum("jtb,ktc->jbkc", sketched, weighted, preferred_element_type=jnp.float32)
    own_cols = own_blocks * width
    block_gram = block_gram.reshape(own_cols, own_cols)
    summed = lax.psum(block_gram, "dp")
    return summed / (lax.axis_size("dp") * tokens * model_width)


ALONG = pl.DeviceIdType.MESH
SPANS = ((0, 2), (2, 4), (4, 6), (6, 7), (7, 8))
CHUNKS = len(SPANS)
FIRST = tuple(sum((hi - lo) * hi for lo, hi in SPANS[:c]) for c in range(CHUNKS + 1))
UNITS = FIRST[CHUNKS]
TRIANGLE = tuple((i, j) for i in range(4) for j in range(i + 1))
GSPANS = ((0, 2), (2, 4), (4, 6), (6, 8), (8, 10))
GS = len(GSPANS)


def pick_kernel(shards, own, per, ids_in, bits_in, grads, out, ids, bits, held, sems):
    z = lax.axis_index("shard")
    width = BLK
    number = shards * own
    cuts = held.shape[0]
    rows = held.shape[1]

    def fetch(n):
        return pltpu.make_async_copy(grads.at[pl.ds(rows * n, rows)], held.at[n], sems.at[n])

    early = (pltpu.make_async_copy(ids_in, ids, sems.at[cuts]), pltpu.make_async_copy(bits_in, bits, sems.at[cuts + 1]))
    for copy in early:
        copy.start()
    for n in range(cuts):
        fetch(n).start()
    for copy in early:
        copy.wait()
    for n in range(cuts):
        fetch(n).wait()

        def take(p, carry):
            block = ids[p // own, lax.rem(p, own)]
            r = block // per
            start = pl.multiple_of((block - r * per) * width, width)
            common = r & z
            odd = common & 1
            for level in range(1, shards.bit_length() - 1):
                odd = odd + ((common >> level) & 1)
            sign = 1 - 2 * (odd & 1)
            flips = (1 - 2 * bits[pl.ds(start, width)].reshape(1, width)) * sign
            flips = flips.astype(jnp.float32).astype(jnp.bfloat16)
            out[p, rows * n : rows * (n + 1)] = held[n, :, pl.ds(start, width)] * flips
            return carry

        lax.fori_loop(0, number, take, 0, unroll=4)


def mix_kernel(
    shards, parts, own, act, picked, out,
    rx, tx, grx, gtx, part, full, sketch, halves, prx, rtx, rrx, gathered,
    z_send, z_recv, p_send, p_recv, r_send, r_recv, f_send, f_recv, a_send, a_recv, w_send, w_recv,
):
    z = lax.axis_index("shard")
    d = lax.axis_index("dp")
    core = lax.rem(d, 2)
    chip = d // 2
    last = shards - 1
    edge = (z == 0) | (z == last)
    middle = jnp.logical_not(edge)
    tokens = act.shape[0]
    width = BLK
    inv_block = 1.0 / math.sqrt(width)
    inv_shard = 1.0 / math.sqrt(shards)
    pieces = 2 * own

    barrier = pltpu.get_barrier_semaphore()

    def peer(m):
        flipped = 1 - lax.rem(chip, 2) if m & 1 else lax.rem(chip, 2)
        high = 1 - chip // 2 if m & 2 else chip // 2
        return (high * 2 + flipped) * 2 + core

    partner = chip * 2 + 1 - core
    for m in (1, 2, 3):
        pl.semaphore_signal(barrier, inc=1, device_id={"dp": peer(m)}, device_id_type=ALONG)
    pl.semaphore_signal(barrier, inc=1, device_id={"dp": partner}, device_id_type=ALONG)

    @pl.when(z > 0)
    def _():
        pl.semaphore_signal(barrier, inc=1, device_id={"shard": z - 1}, device_id_type=ALONG)

    @pl.when(z < last)
    def _():
        pl.semaphore_signal(barrier, inc=1, device_id={"shard": z + 1}, device_id_type=ALONG)

    row = lax.broadcasted_iota(jnp.int32, (width, width), 0)
    col = lax.broadcasted_iota(jnp.int32, (width, width), 1)
    both = row & col
    count = both & 1
    for level in range(1, width.bit_length() - 1):
        count = count + ((both >> level) & 1)
    table = (1 - 2 * (count & 1)).astype(jnp.float32).astype(jnp.bfloat16)

    def contribution(owner, j):
        lm = jnp.dot(picked[owner * own + j], table, preferred_element_type=jnp.float32)
        return (lm * inv_block).astype(jnp.bfloat16).astype(jnp.float32) * inv_shard

    def owner_of(way, t):
        return jnp.where(way == 0, 1 - t, 2 + t)

    def target(way):
        return jnp.where(way == 0, z - 1, z + 1)

    half = tokens // 2

    def s_move(way, k, h, who):
        rows = pl.ds(half * h, half)
        return pltpu.make_async_remote_copy(
            tx.at[way, k, rows], rx.at[way, k, rows], z_send.at[way, GS + 2 * k + h], z_recv.at[way, GS + 2 * k + h],
            device_id={"shard": who}, device_id_type=ALONG)

    def s_copy(way, k, h):
        return s_move(way, k, h, target(way))

    def g_copy(way, i):
        lo, hi = GSPANS[i]
        return pltpu.make_async_remote_copy(
            gtx.at[way, lo:hi], grx.at[way, lo:hi], z_send.at[way, i], z_recv.at[way, i],
            device_id={"shard": target(way)}, device_id_type=ALONG)

    def gpart(n):
        i, j = TRIANGLE[n]
        return part[128 * i : 128 * (i + 1), 128 * j : 128 * (j + 1)]

    def units(c):
        return pl.ds(FIRST[c], FIRST[c + 1] - FIRST[c])

    def a_copy(c, slot, who):
        return pltpu.make_async_remote_copy(
            gathered.at[d, units(c)], gathered.at[d, units(c)], a_send.at[c, slot], a_recv.at[c, slot],
            device_id={"dp": who}, device_id_type=ALONG)

    def a_recv_from(c, slot, who):
        return pltpu.make_async_remote_copy(
            gathered.at[who, units(c)], gathered.at[who, units(c)], a_send.at[c, slot], a_recv.at[c, slot],
            device_id={"dp": who}, device_id_type=ALONG)

    def w_copy(c, m):
        return pltpu.make_async_remote_copy(
            gathered.at[peer(m), units(c)], gathered.at[peer(m), units(c)],
            w_send.at[c, m - 1], w_recv.at[c, m - 1],
            device_id={"dp": partner}, device_id_type=ALONG)

    def w_recv_from(c, m):
        other = peer(m) + 1 - 2 * core
        return pltpu.make_async_remote_copy(
            gathered.at[other, units(c)], gathered.at[other, units(c)],
            w_send.at[c, m - 1], w_recv.at[c, m - 1],
            device_id={"dp": partner}, device_id_type=ALONG)

    def spread(c):
        for m in (1, 2, 3):
            a_copy(c, m - 1, peer(m)).start()
        a_copy(c, 3, partner).start()

    def relay(c):
        for m in (1, 2, 3):
            a_recv_from(c, m - 1, peer(m)).wait_recv()
            w_copy(c, m).start()

    def settle(c):
        a_recv_from(c, 3, partner).wait_recv()
        for m in (1, 2, 3):
            w_recv_from(c, m).wait_recv()
        for m in (1, 2, 3):
            a_copy(c, m - 1, peer(m)).wait_send()
            w_copy(c, m).wait_send()
        a_copy(c, 3, partner).wait_send()

    def f_copy(c):
        inward = jnp.where(z == 0, 1, last - 1)
        return pltpu.make_async_remote_copy(
            rrx.at[3, units(c)], gathered.at[d, units(c)], f_send.at[c], f_recv.at[c],
            device_id={"shard": inward}, device_id_type=ALONG)

    def f_recv_at():
        def make(c):
            outward = jnp.where(z == 1, 0, last)
            return pltpu.make_async_remote_copy(
                rrx.at[3, units(c)], gathered.at[d, units(c)], f_send.at[c], f_recv.at[c],
                device_id={"shard": outward}, device_id_type=ALONG)
        return make

    part[...] = lax.dot_general(act[...], act[...], (((1,), (1,)), ((), ())), preferred_element_type=jnp.float32)

    @pl.when(edge)
    def _():
        pl.semaphore_wait(barrier, 5)

    @pl.when(middle)
    def _():
        pl.semaphore_wait(barrier, 6)

    @pl.when(edge)
    def _():
        out_way = jnp.where(z == 0, 1, 0)
        in_way = 1 - out_way
        for i in range(GS):
            for n in range(*GSPANS[i]):
                gtx[out_way, n] = gpart(n).astype(jnp.bfloat16)
            g_copy(out_way, i).start()

        def push(k, carry):
            t, j = k // own, lax.rem(k, own)
            tx[out_way, k] = contribution(owner_of(out_way, t), j).astype(jnp.bfloat16)
            for h in range(2):
                s_copy(out_way, k, h).start()
            return carry

        lax.fori_loop(0, pieces, push, 0)

        for i in range(GS):
            lo, hi = GSPANS[i]
            pltpu.make_async_remote_copy(
                gtx.at[in_way, lo:hi], grx.at[in_way, lo:hi], z_send.at[in_way, i], z_recv.at[in_way, i],
                device_id={"shard": target(out_way)}, device_id_type=ALONG).wait_recv()
            for n in range(lo, hi):
                r, c = TRIANGLE[n]
                block = (grx[in_way, n].astype(jnp.float32) + gpart(n)).astype(jnp.bfloat16)
                full[128 * r : 128 * (r + 1), 128 * c : 128 * (c + 1)] = block
                if r != c:
                    full[128 * c : 128 * (c + 1), 128 * r : 128 * (r + 1)] = block.T

        def where(q):
            t, c = q // CHUNKS, q % CHUNKS
            return t, c, pl.ds(UNITS * t + FIRST[c], FIRST[c + 1] - FIRST[c])

        def p_copy(q):
            t, c, us = where(q)
            return pltpu.make_async_remote_copy(
                halves.at[1 - core, us], prx.at[us], p_send.at[q], p_recv.at[q],
                device_id={"dp": partner}, device_id_type=ALONG)

        def r_copy(q, m):
            t, c, us = where(q)
            return pltpu.make_async_remote_copy(
                rtx.at[peer(m) // 2, us], rrx.at[m - 1, us], r_send.at[q, m - 1], r_recv.at[q, m - 1],
                device_id={"dp": peer(m)}, device_id_type=ALONG)

        def step_a(q):
            t, c, us = where(q)
            lo, hi = SPANS[c]
            for j in range(lo, hi):
                k = own * t + j
                mine = contribution(owner_of(in_way, t), j)
                for h in range(2):
                    s_move(in_way, k, h, target(out_way)).wait_recv()
                done = (rx[in_way, k].astype(jnp.float32) + mine).astype(jnp.bfloat16)
                sketch[t, :, width * j : width * (j + 1)] = done
            cols = sketch[t, :, width * lo : width * hi]
            weighted = jnp.dot(full[...], cols, preferred_element_type=jnp.float32).astype(jnp.bfloat16)
            for top in range(0, hi, 2):
                end = min(top + 2, hi)
                unit = lax.dot_general(
                    sketch[t, :, width * top : width * end], weighted, (((0,), (0,)), ((), ())),
                    preferred_element_type=jnp.float32)
                for i in range(top, end):
                    for j in range(lo, hi):
                        u = UNITS * t + FIRST[c] + (j - lo) * hi + i
                        block = unit[128 * (i - top) : 128 * (i - top + 1), width * (j - lo) : width * (j - lo + 1)]
                        halves[0, u] = block[:64]
                        halves[1, u] = block[64:]
            p_copy(q).start()

        def step_b(q):
            t, c, us = where(q)
            p_copy(q).wait_recv()
            total = (halves[core, us] + prx[us]).astype(jnp.bfloat16)
            for n in range(4):
                rtx[n, us] = total[:, 16 * n : 16 * (n + 1)]
            for m in (1, 2, 3):
                r_copy(q, m).start()

        def step_c(q):
            t, c, us = where(q)
            for m in (1, 2, 3):
                r_copy(q, m).wait_recv()
            total = rtx[chip, us].astype(jnp.float32)
            for m in range(3):
                total = total + rrx[m, us].astype(jnp.float32)
            total = (total * (1.0 / (parts * tokens * act.shape[1] * shards))).astype(jnp.bfloat16)
            if t == 0:
                rrx[3, units(c)] = total
            else:
                gathered[d, units(c)] = total
            if t == 0:
                f_copy(c).start()
            else:
                spread(c)

        def step_d(q):
            if q >= CHUNKS:
                relay(q - CHUNKS)

        steps = 2 * CHUNKS
        for q in range(steps + 3):
            if 0 <= q - 1 < steps:
                step_b(q - 1)
            if 0 <= q - 2 < steps:
                step_c(q - 2)
            if 0 <= q - 3 < steps:
                step_d(q - 3)
            if q < steps:
                step_a(q)
        for c in range(CHUNKS):
            settle(c)
            f_copy(c).wait_send()
        for q in range(steps):
            p_copy(q).wait_send()
            for m in (1, 2, 3):
                r_copy(q, m).wait_send()
        for i in range(GS):
            g_copy(out_way, i).wait_send()

        def drain(k, carry):
            for h in range(2):
                s_copy(out_way, k, h).wait_send()
            return carry

        lax.fori_loop(0, pieces, drain, 0)

    @pl.when(middle)
    def _():
        near = jnp.where(z == 1, 1, 0)
        far = 1 - near

        def pass_g(way, i):
            g_copy(way, i).wait_recv()
            for n in range(*GSPANS[i]):
                gtx[way, n] = (grx[way, n].astype(jnp.float32) + gpart(n)).astype(jnp.bfloat16)
            g_copy(way, i).start()

        def pass_s(way, k):
            t, j = k // own, lax.rem(k, own)
            mine = contribution(owner_of(way, t), j)
            for h in range(2):
                s_copy(way, k, h).wait_recv()
                rows = slice(half * h, half * (h + 1))
                tx[way, k, rows] = (rx[way, k, rows].astype(jnp.float32) + mine[rows]).astype(jnp.bfloat16)
                s_copy(way, k, h).start()

        for i in range(GS):
            pass_g(near, i)
            if i >= 2:
                pass_g(far, i - 2)
        pass_s(near, 0)
        pass_g(far, GS - 2)
        pass_g(far, GS - 1)

        def both_ways(k, carry):
            pass_s(near, k)
            pass_s(far, k - 1)
            return carry

        lax.fori_loop(1, pieces, both_ways, 0)
        pass_s(far, pieces - 1)
        arrival = f_recv_at()
        for c in range(CHUNKS):
            arrival(c).wait_recv()
            spread(c)
        for c in range(CHUNKS):
            relay(c)
        for c in range(CHUNKS):
            settle(c)
        for way in range(2):
            for i in range(GS):
                g_copy(way, i).wait_send()

        def drain(k, carry):
            for way in range(2):
                for h in range(2):
                    s_copy(way, k, h).wait_send()
            return carry

        lax.fori_loop(0, pieces, drain, 0)

    out[...] = gathered[...]


def assemble_kernel(got, out, held, sems):
    chunk_of = [c for c, (lo, hi) in enumerate(SPANS) for _ in range(lo, hi)]

    def unit(i, j):
        c = chunk_of[j]
        lo, hi = SPANS[c]
        u = FIRST[c] + (j - lo) * hi + i
        rows = [got[2 * n + h, u] for h in range(2) for n in range(4)]
        return jnp.concatenate(rows, axis=0).astype(jnp.float32)

    count = len(chunk_of)

    def put(i):
        rows = pl.ds(BLK * i, BLK)
        return pltpu.make_async_copy(held.at[rows], out.at[rows], sems.at[i])

    for i in range(count):
        for j in range(count):
            block = unit(i, j) if i < SPANS[chunk_of[j]][1] else unit(j, i).T
            held[BLK * i : BLK * (i + 1), BLK * j : BLK * (j + 1)] = block
        put(i).start()
    for i in range(count):
        put(i).wait()


def fast_body(shards, parts, activations, out_grads, sign_bits, block_ids):
    tokens, columns = out_grads.shape
    per = columns // BLK
    own = block_ids.shape[1]
    vmem = pl.BlockSpec(memory_space=pltpu.VMEM)
    bf, f32 = jnp.bfloat16, jnp.float32
    dma = pltpu.SemaphoreType.DMA
    number = shards * own
    hbm = pl.BlockSpec(memory_space=pltpu.HBM)
    picked = pl.pallas_call(
        functools.partial(pick_kernel, shards, own, per),
        out_shape=jax.ShapeDtypeStruct((number, tokens, BLK), bf),
        in_specs=[hbm, hbm, hbm],
        out_specs=vmem,
        scratch_shapes=[
            pltpu.SMEM(block_ids.shape, jnp.int32),
            pltpu.VMEM((columns,), jnp.int32),
            pltpu.VMEM((4, tokens // 4, columns), bf),
            dma((6,)),
        ],
        compiler_params=pltpu.CompilerParams(vmem_limit_bytes=12 * 2**20),
        name="pick",
    )(block_ids, sign_bits, out_grads)
    got = pl.pallas_call(
        functools.partial(mix_kernel, shards, parts, own),
        out_shape=jax.ShapeDtypeStruct((parts, UNITS, 16, BLK), bf),
        in_specs=[vmem, vmem],
        out_specs=vmem,
        scratch_shapes=[
            pltpu.VMEM((2, 2 * own, tokens, BLK), bf),
            pltpu.VMEM((2, 2 * own, tokens, BLK), bf),
            pltpu.VMEM((2, 10, 128, 128), bf),
            pltpu.VMEM((2, 10, 128, 128), bf),
            pltpu.VMEM((tokens, tokens), f32),
            pltpu.VMEM((tokens, tokens), bf),
            pltpu.VMEM((2, tokens, own * BLK), bf),
            pltpu.VMEM((2, 2 * UNITS, 64, BLK), f32),
            pltpu.VMEM((2 * UNITS, 64, BLK), f32),
            pltpu.VMEM((4, 2 * UNITS, 16, BLK), bf),
            pltpu.VMEM((4, 2 * UNITS, 16, BLK), bf),
            pltpu.VMEM((parts, UNITS, 16, BLK), bf),
            dma((2, GS + 4 * own)), dma((2, GS + 4 * own)),
            dma((2 * CHUNKS,)), dma((2 * CHUNKS,)),
            dma((2 * CHUNKS, 3)), dma((2 * CHUNKS, 3)),
            dma((CHUNKS,)), dma((CHUNKS,)),
            dma((CHUNKS, 4)), dma((CHUNKS, 4)),
            dma((CHUNKS, 3)), dma((CHUNKS, 3)),
        ],
        compiler_params=pltpu.CompilerParams(collective_id=0, has_side_effects=True, vmem_limit_bytes=40 * 2**20),
        name="mix",
    )(activations, picked)
    return pl.pallas_call(
        assemble_kernel,
        out_shape=jax.ShapeDtypeStruct((own * BLK, own * BLK), f32),
        in_specs=[vmem],
        out_specs=hbm,
        scratch_shapes=[pltpu.VMEM((own * BLK, own * BLK), f32), dma((own,))],
        compiler_params=pltpu.CompilerParams(vmem_limit_bytes=16 * 2**20),
        name="assemble",
    )(got)


def solution(mesh):
    in_specs = (P("dp", "shard"), P("dp", "shard"), P("shard"), P())
    out_specs = P("shard", None)
    shards, parts = mesh.shape["shard"], mesh.shape["dp"]
    chosen = functools.partial(fast_body, shards, parts) if (shards, parts) == (4, 8) else body
    return jax.shard_map(chosen, mesh=mesh, in_specs=in_specs, out_specs=out_specs, check_vma=False)
```

```python
import functools
import math

import jax
import jax.numpy as jnp
from jax import lax
from jax.experimental import pallas as pl
from jax.experimental.pallas import tpu as pltpu
from jax.sharding import PartitionSpec as P

BLK = 128
CAP = 2


def partner_2(x, axis, distance):
    return lax.ppermute(x, axis, [(i, i ^ 1 << distance) for i in range(lax.axis_size(axis))])


def parity_table(count):
    index = jnp.arange(count, dtype=jnp.int32)
    total = jnp.zeros((count, count), jnp.int32)
    for level in range(count.bit_length() - 1):
        total = total + (
            jnp.right_shift(index[:, None], level) & jnp.right_shift(index[None, :], level) & 1
        )
    return (1 - 2 * (total % 2)).astype(jnp.float32)


def route_sampled(mixed, block_ids, me_index, shards, blocks_per, tokens, width):
    groups = block_ids.shape[1] // CAP
    sources = block_ids[:, ::CAP] // blocks_per
    local_ids = (block_ids % blocks_per).reshape(shards, groups, CAP)
    matched = sources == me_index
    chosen = jnp.sum(jnp.where(matched[:, :, None], local_ids, 0), axis=1)
    live_rows = jnp.any(matched, axis=1).astype(jnp.bfloat16)
    outgoing = jnp.take(mixed, chosen.reshape(-1), axis=0).reshape(shards, CAP, tokens, width)
    return (outgoing * live_rows[:, None, None, None], jnp.take(sources, me_index, axis=0))


def body(activations, out_grads, sign_bits, block_ids):
    shards = lax.axis_size("shard")
    me_index = lax.axis_index("shard")
    tokens = out_grads.shape[0]
    width = BLK
    own_blocks = block_ids.shape[1]
    blocks_per = out_grads.shape[1] // width
    model_width = activations.shape[1] * shards
    inv_block = 1.0 / math.sqrt(width)
    inv_shard = 1.0 / math.sqrt(shards)
    partial_gram = jnp.dot(activations, activations.T, preferred_element_type=jnp.float32)
    token_gram = lax.psum(partial_gram, "shard").astype(jnp.bfloat16)
    sign_values = (1 - 2 * sign_bits).astype(jnp.bfloat16)
    flipped = (out_grads * sign_values[None, :]).reshape(tokens, blocks_per, width)
    block_table = parity_table(width).astype(jnp.bfloat16)
    local_mix = jnp.einsum("tbj,jk->btk", flipped, block_table, preferred_element_type=jnp.float32)
    local_mix = (local_mix * inv_block).astype(jnp.bfloat16)
    running = local_mix.astype(jnp.float32)
    for level in range(shards.bit_length() - 1):
        partner = partner_2(running, "shard", level)
        upper = jnp.right_shift(me_index, level) & 1 == 1
        running = jnp.where(upper, partner - running, running + partner)
    mixed = (running * inv_shard).astype(jnp.bfloat16)
    outgoing, own_sources = route_sampled(
        mixed, block_ids, me_index, shards, blocks_per, tokens, width
    )
    incoming = lax.all_to_all(outgoing, "shard", split_axis=0, concat_axis=0, tiled=True)
    sketched = jnp.take(incoming, own_sources, axis=0).reshape(own_blocks, tokens, width)
    weighted = jnp.einsum(
        "tu,jub->jtb", token_gram, sketched, preferred_element_type=jnp.float32
    ).astype(jnp.bfloat16)
    block_gram = jnp.einsum("jtb,ktc->jbkc", sketched, weighted, preferred_element_type=jnp.float32)
    own_cols = own_blocks * width
    block_gram = block_gram.reshape(own_cols, own_cols)
    summed = lax.psum(block_gram, "dp")
    return summed / (lax.axis_size("dp") * tokens * model_width)


ALONG = pl.DeviceIdType.MESH
SPANS = ((0, 2), (2, 4), (4, 6), (6, 7), (7, 8))
CHUNKS = len(SPANS)
FIRST = tuple(sum((hi - lo) * hi for lo, hi in SPANS[:c]) for c in range(CHUNKS + 1))
UNITS = FIRST[CHUNKS]
TRIANGLE = tuple((i, j) for i in range(4) for j in range(i + 1))
GSPANS = ((0, 2), (2, 4), (4, 6), (6, 8), (8, 10))
GS = len(GSPANS)
CUTS = 4


def pick_kernel(shards, own, per, ids, bits, grads, out):
    z = lax.axis_index("shard")
    width = BLK
    number = shards * own

    def start_of(p):
        block = ids[p // own, lax.rem(p, own)]
        r = block // per
        return r, pl.multiple_of((block - r * per) * width, width)

    def take(p, carry):
        r, start = start_of(p)
        common = r & z
        odd = common & 1
        for level in range(1, shards.bit_length() - 1):
            odd = odd + ((common >> level) & 1)
        sign = 1 - 2 * (odd & 1)
        signs = ((1 - 2 * bits[pl.ds(start, width)].reshape(1, width)) * sign).astype(jnp.float32).astype(jnp.bfloat16)
        out[p] = grads[:, pl.ds(start, width)] * signs
        return carry

    lax.fori_loop(0, number, take, 0, unroll=4)


def mix_kernel(
    shards, parts, own, act, picked, out,
    rx, tx, grx, gtx, part, full, sketch, halves, prx, rtx, rrx, gathered,
    z_send, z_recv, p_send, p_recv, r_send, r_recv, f_send, f_recv, a_send, a_recv, w_send, w_recv,
):
    z = lax.axis_index("shard")
    d = lax.axis_index("dp")
    core = lax.rem(d, 2)
    chip = d // 2
    last = shards - 1
    edge = (z == 0) | (z == last)
    middle = jnp.logical_not(edge)
    tokens = act.shape[0]
    width = BLK
    inv_block = 1.0 / math.sqrt(width)
    inv_shard = 1.0 / math.sqrt(shards)
    pieces = 2 * own

    barrier = pltpu.get_barrier_semaphore()

    def peer(m):
        flipped = 1 - lax.rem(chip, 2) if m & 1 else lax.rem(chip, 2)
        high = 1 - chip // 2 if m & 2 else chip // 2
        return (high * 2 + flipped) * 2 + core

    partner = chip * 2 + 1 - core
    for m in (1, 2, 3):
        pl.semaphore_signal(barrier, inc=1, device_id={"dp": peer(m)}, device_id_type=ALONG)
    pl.semaphore_signal(barrier, inc=1, device_id={"dp": partner}, device_id_type=ALONG)

    @pl.when(z > 0)
    def _():
        pl.semaphore_signal(barrier, inc=1, device_id={"shard": z - 1}, device_id_type=ALONG)

    @pl.when(z < last)
    def _():
        pl.semaphore_signal(barrier, inc=1, device_id={"shard": z + 1}, device_id_type=ALONG)

    row = lax.broadcasted_iota(jnp.int32, (width, width), 0)
    col = lax.broadcasted_iota(jnp.int32, (width, width), 1)
    both = row & col
    count = both & 1
    for level in range(1, width.bit_length() - 1):
        count = count + ((both >> level) & 1)
    table = (1 - 2 * (count & 1)).astype(jnp.float32).astype(jnp.bfloat16)

    def contribution(owner, j):
        lm = jnp.dot(picked[owner * own + j], table, preferred_element_type=jnp.float32)
        return (lm * inv_block).astype(jnp.bfloat16).astype(jnp.float32) * inv_shard

    def owner_of(way, t):
        return jnp.where(way == 0, 1 - t, 2 + t)

    def target(way):
        return jnp.where(way == 0, z - 1, z + 1)

    half = tokens // CUTS

    def s_move(way, k, h, who):
        rows = pl.ds(half * h, half)
        return pltpu.make_async_remote_copy(
            tx.at[way, k, rows], rx.at[way, k, rows], z_send.at[way, GS + CUTS * k + h], z_recv.at[way, GS + CUTS * k + h],
            device_id={"shard": who}, device_id_type=ALONG)

    def s_copy(way, k, h):
        return s_move(way, k, h, target(way))

    def g_copy(way, i):
        lo, hi = GSPANS[i]
        return pltpu.make_async_remote_copy(
            gtx.at[way, lo:hi], grx.at[way, lo:hi], z_send.at[way, i], z_recv.at[way, i],
            device_id={"shard": target(way)}, device_id_type=ALONG)

    def gpart(n):
        i, j = TRIANGLE[n]
        return part[128 * i : 128 * (i + 1), 128 * j : 128 * (j + 1)]

    def units(c):
        return pl.ds(FIRST[c], FIRST[c + 1] - FIRST[c])

    def a_copy(c, slot, who):
        return pltpu.make_async_remote_copy(
            gathered.at[d, units(c)], gathered.at[d, units(c)], a_send.at[c, slot], a_recv.at[c, slot],
            device_id={"dp": who}, device_id_type=ALONG)

    def a_recv_from(c, slot, who):
        return pltpu.make_async_remote_copy(
            gathered.at[who, units(c)], gathered.at[who, units(c)], a_send.at[c, slot], a_recv.at[c, slot],
            device_id={"dp": who}, device_id_type=ALONG)

    def w_copy(c, m):
        return pltpu.make_async_remote_copy(
            gathered.at[peer(m), units(c)], gathered.at[peer(m), units(c)],
            w_send.at[c, m - 1], w_recv.at[c, m - 1],
            device_id={"dp": partner}, device_id_type=ALONG)

    def w_recv_from(c, m):
        other = peer(m) + 1 - 2 * core
        return pltpu.make_async_remote_copy(
            gathered.at[other, units(c)], gathered.at[other, units(c)],
            w_send.at[c, m - 1], w_recv.at[c, m - 1],
            device_id={"dp": partner}, device_id_type=ALONG)

    def spread(c):
        for m in (1, 2, 3):
            a_copy(c, m - 1, peer(m)).start()
        a_copy(c, 3, partner).start()

    def relay(c):
        for m in (1, 2, 3):
            a_recv_from(c, m - 1, peer(m)).wait_recv()
            w_copy(c, m).start()

    def settle(c):
        a_recv_from(c, 3, partner).wait_recv()
        for m in (1, 2, 3):
            w_recv_from(c, m).wait_recv()
        for m in (1, 2, 3):
            a_copy(c, m - 1, peer(m)).wait_send()
            w_copy(c, m).wait_send()
        a_copy(c, 3, partner).wait_send()

    def f_copy(c):
        inward = jnp.where(z == 0, 1, last - 1)
        return pltpu.make_async_remote_copy(
            rrx.at[3, units(c)], gathered.at[d, units(c)], f_send.at[c], f_recv.at[c],
            device_id={"shard": inward}, device_id_type=ALONG)

    def f_recv_at():
        def make(c):
            outward = jnp.where(z == 1, 0, last)
            return pltpu.make_async_remote_copy(
                rrx.at[3, units(c)], gathered.at[d, units(c)], f_send.at[c], f_recv.at[c],
                device_id={"shard": outward}, device_id_type=ALONG)
        return make

    part[...] = lax.dot_general(act[...], act[...], (((1,), (1,)), ((), ())), preferred_element_type=jnp.float32)

    @pl.when(edge)
    def _():
        pl.semaphore_wait(barrier, 5)

    @pl.when(middle)
    def _():
        pl.semaphore_wait(barrier, 6)

    @pl.when(edge)
    def _():
        out_way = jnp.where(z == 0, 1, 0)
        in_way = 1 - out_way
        for i in range(GS):
            for n in range(*GSPANS[i]):
                gtx[out_way, n] = gpart(n).astype(jnp.bfloat16)
            g_copy(out_way, i).start()

        def push(k, carry):
            t, j = k // own, lax.rem(k, own)
            tx[out_way, k] = contribution(owner_of(out_way, t), j).astype(jnp.bfloat16)
            for h in range(CUTS):
                s_copy(out_way, k, h).start()
            return carry

        lax.fori_loop(0, pieces, push, 0)

        for i in range(GS):
            lo, hi = GSPANS[i]
            pltpu.make_async_remote_copy(
                gtx.at[in_way, lo:hi], grx.at[in_way, lo:hi], z_send.at[in_way, i], z_recv.at[in_way, i],
                device_id={"shard": target(out_way)}, device_id_type=ALONG).wait_recv()
            for n in range(lo, hi):
                r, c = TRIANGLE[n]
                block = (grx[in_way, n].astype(jnp.float32) + gpart(n)).astype(jnp.bfloat16)
                full[128 * r : 128 * (r + 1), 128 * c : 128 * (c + 1)] = block
                if r != c:
                    full[128 * c : 128 * (c + 1), 128 * r : 128 * (r + 1)] = block.T

        def where(q):
            t, c = q // CHUNKS, q % CHUNKS
            return t, c, pl.ds(UNITS * t + FIRST[c], FIRST[c + 1] - FIRST[c])

        def p_copy(q):
            t, c, us = where(q)
            return pltpu.make_async_remote_copy(
                halves.at[1 - core, us], prx.at[us], p_send.at[q], p_recv.at[q],
                device_id={"dp": partner}, device_id_type=ALONG)

        def r_copy(q, m):
            t, c, us = where(q)
            return pltpu.make_async_remote_copy(
                rtx.at[peer(m) // 2, us], rrx.at[m - 1, us], r_send.at[q, m - 1], r_recv.at[q, m - 1],
                device_id={"dp": peer(m)}, device_id_type=ALONG)

        def step_a(q):
            t, c, us = where(q)
            lo, hi = SPANS[c]
            for j in range(lo, hi):
                k = own * t + j
                mine = contribution(owner_of(in_way, t), j)
                for h in range(CUTS):
                    s_move(in_way, k, h, target(out_way)).wait_recv()
                done = (rx[in_way, k].astype(jnp.float32) + mine).astype(jnp.bfloat16)
                sketch[t, :, width * j : width * (j + 1)] = done
            cols = sketch[t, :, width * lo : width * hi]
            weighted = jnp.dot(full[...], cols, preferred_element_type=jnp.float32).astype(jnp.bfloat16)
            for top in range(0, hi, 2):
                end = min(top + 2, hi)
                unit = lax.dot_general(
                    sketch[t, :, width * top : width * end], weighted, (((0,), (0,)), ((), ())),
                    preferred_element_type=jnp.float32)
                for i in range(top, end):
                    for j in range(lo, hi):
                        u = UNITS * t + FIRST[c] + (j - lo) * hi + i
                        block = unit[128 * (i - top) : 128 * (i - top + 1), width * (j - lo) : width * (j - lo + 1)]
                        halves[0, u] = block[:64]
                        halves[1, u] = block[64:]
            p_copy(q).start()

        def step_b(q):
            t, c, us = where(q)
            p_copy(q).wait_recv()
            total = (halves[core, us] + prx[us]).astype(jnp.bfloat16)
            for n in range(4):
                rtx[n, us] = total[:, 16 * n : 16 * (n + 1)]
            for m in (1, 2, 3):
                r_copy(q, m).start()

        def step_c(q):
            t, c, us = where(q)
            for m in (1, 2, 3):
                r_copy(q, m).wait_recv()
            total = rtx[chip, us].astype(jnp.float32)
            for m in range(3):
                total = total + rrx[m, us].astype(jnp.float32)
            total = (total * (1.0 / (parts * tokens * act.shape[1] * shards))).astype(jnp.bfloat16)
            if t == 0:
                rrx[3, units(c)] = total
            else:
                gathered[d, units(c)] = total
            if t == 0:
                f_copy(c).start()
            else:
                spread(c)

        def step_d(q):
            if q >= CHUNKS:
                relay(q - CHUNKS)

        steps = 2 * CHUNKS
        for q in range(steps + 3):
            if 0 <= q - 1 < steps:
                step_b(q - 1)
            if 0 <= q - 2 < steps:
                step_c(q - 2)
            if 0 <= q - 3 < steps:
                step_d(q - 3)
            if q < steps:
                step_a(q)
        for c in range(CHUNKS):
            settle(c)
            f_copy(c).wait_send()
        for q in range(steps):
            p_copy(q).wait_send()
            for m in (1, 2, 3):
                r_copy(q, m).wait_send()
        for i in range(GS):
            g_copy(out_way, i).wait_send()

        def drain(k, carry):
            for h in range(CUTS):
                s_copy(out_way, k, h).wait_send()
            return carry

        lax.fori_loop(0, pieces, drain, 0)

    @pl.when(middle)
    def _():
        near = jnp.where(z == 1, 1, 0)
        far = 1 - near

        def pass_g(way, i):
            g_copy(way, i).wait_recv()
            for n in range(*GSPANS[i]):
                gtx[way, n] = (grx[way, n].astype(jnp.float32) + gpart(n)).astype(jnp.bfloat16)
            g_copy(way, i).start()

        def pass_s(way, k):
            t, j = k // own, lax.rem(k, own)
            mine = contribution(owner_of(way, t), j)
            for h in range(CUTS):
                s_copy(way, k, h).wait_recv()
                rows = slice(half * h, half * (h + 1))
                tx[way, k, rows] = (rx[way, k, rows].astype(jnp.float32) + mine[rows]).astype(jnp.bfloat16)
                s_copy(way, k, h).start()

        for i in range(GS):
            pass_g(near, i)
            if i >= 2:
                pass_g(far, i - 2)
        pass_s(near, 0)
        pass_g(far, GS - 2)
        pass_g(far, GS - 1)

        def both_ways(k, carry):
            pass_s(near, k)
            pass_s(far, k - 1)
            return carry

        lax.fori_loop(1, pieces, both_ways, 0)
        pass_s(far, pieces - 1)
        arrival = f_recv_at()
        for c in range(CHUNKS):
            arrival(c).wait_recv()
            spread(c)
        for c in range(CHUNKS):
            relay(c)
        for c in range(CHUNKS):
            settle(c)
        for way in range(2):
            for i in range(GS):
                g_copy(way, i).wait_send()

        def drain(k, carry):
            for way in range(2):
                for h in range(CUTS):
                    s_copy(way, k, h).wait_send()
            return carry

        lax.fori_loop(0, pieces, drain, 0)

    out[...] = gathered[...]


def assemble_kernel(got, out, held, sems):
    chunk_of = [c for c, (lo, hi) in enumerate(SPANS) for _ in range(lo, hi)]

    def unit(i, j):
        c = chunk_of[j]
        lo, hi = SPANS[c]
        u = FIRST[c] + (j - lo) * hi + i
        rows = [got[2 * n + h, u] for h in range(2) for n in range(4)]
        return jnp.concatenate(rows, axis=0).astype(jnp.float32)

    count = len(chunk_of)

    def put(i):
        rows = pl.ds(BLK * i, BLK)
        return pltpu.make_async_copy(held.at[rows], out.at[rows], sems.at[i])

    for i in range(count):
        for j in range(count):
            block = unit(i, j) if i < SPANS[chunk_of[j]][1] else unit(j, i).T
            held[BLK * i : BLK * (i + 1), BLK * j : BLK * (j + 1)] = block
        put(i).start()
    for i in range(count):
        put(i).wait()


def fast_body(shards, parts, activations, out_grads, sign_bits, block_ids):
    tokens, columns = out_grads.shape
    per = columns // BLK
    own = block_ids.shape[1]
    vmem = pl.BlockSpec(memory_space=pltpu.VMEM)
    bf, f32 = jnp.bfloat16, jnp.float32
    dma = pltpu.SemaphoreType.DMA
    number = shards * own
    hbm = pl.BlockSpec(memory_space=pltpu.HBM)
    picked = pl.pallas_call(
        functools.partial(pick_kernel, shards, own, per),
        out_shape=jax.ShapeDtypeStruct((number, tokens, BLK), bf),
        in_specs=[pl.BlockSpec(memory_space=pltpu.SMEM), vmem, vmem],
        out_specs=vmem,
        compiler_params=pltpu.CompilerParams(vmem_limit_bytes=12 * 2**20),
        name="pick",
    )(block_ids, sign_bits, out_grads)
    got = pl.pallas_call(
        functools.partial(mix_kernel, shards, parts, own),
        out_shape=jax.ShapeDtypeStruct((parts, UNITS, 16, BLK), bf),
        in_specs=[vmem, vmem],
        out_specs=vmem,
        scratch_shapes=[
            pltpu.VMEM((2, 2 * own, tokens, BLK), bf),
            pltpu.VMEM((2, 2 * own, tokens, BLK), bf),
            pltpu.VMEM((2, 10, 128, 128), bf),
            pltpu.VMEM((2, 10, 128, 128), bf),
            pltpu.VMEM((tokens, tokens), f32),
            pltpu.VMEM((tokens, tokens), bf),
            pltpu.VMEM((2, tokens, own * BLK), bf),
            pltpu.VMEM((2, 2 * UNITS, 64, BLK), f32),
            pltpu.VMEM((2 * UNITS, 64, BLK), f32),
            pltpu.VMEM((4, 2 * UNITS, 16, BLK), bf),
            pltpu.VMEM((4, 2 * UNITS, 16, BLK), bf),
            pltpu.VMEM((parts, UNITS, 16, BLK), bf),
            dma((2, GS + 2 * CUTS * own)), dma((2, GS + 2 * CUTS * own)),
            dma((2 * CHUNKS,)), dma((2 * CHUNKS,)),
            dma((2 * CHUNKS, 3)), dma((2 * CHUNKS, 3)),
            dma((CHUNKS,)), dma((CHUNKS,)),
            dma((CHUNKS, 4)), dma((CHUNKS, 4)),
            dma((CHUNKS, 3)), dma((CHUNKS, 3)),
        ],
        compiler_params=pltpu.CompilerParams(collective_id=0, has_side_effects=True, vmem_limit_bytes=40 * 2**20),
        name="mix",
    )(activations, picked)
    return pl.pallas_call(
        assemble_kernel,
        out_shape=jax.ShapeDtypeStruct((own * BLK, own * BLK), f32),
        in_specs=[vmem],
        out_specs=hbm,
        scratch_shapes=[pltpu.VMEM((own * BLK, own * BLK), f32), dma((own,))],
        compiler_params=pltpu.CompilerParams(vmem_limit_bytes=16 * 2**20),
        name="assemble",
    )(got)


def solution(mesh):
    in_specs = (P("dp", "shard"), P("dp", "shard"), P("shard"), P())
    out_specs = P("shard", None)
    shards, parts = mesh.shape["shard"], mesh.shape["dp"]
    chosen = functools.partial(fast_body, shards, parts) if (shards, parts) == (4, 8) else body
    return jax.shard_map(chosen, mesh=mesh, in_specs=in_specs, out_specs=out_specs, check_vma=False)
```
